32 devices in a mesh: shard: 4 (over z), ctx: 4 (over x, core), tp: 2 (over y).
Axes of the slice: x: 2, y: 2, z: 4, core: 2. Of those that a mesh axis runs over, the one named last changes fastest.
Arguments:
- hidden_in: bfloat16 [4, 1024, 1024], P('shard', 'ctx'), may hold values from -6 to 6
- out_grad: bfloat16 [4, 1024, 1024], P('shard', 'ctx'), may hold values from -6 to 6
- segment_ids: int32 [4, 1024], P('shard'), may hold values from 0 to 3, never falling along the last dimension, each value on 1 to 512 neighbouring positions
- w_qkv: bfloat16 [3, 1024, 1024], P(None, 'shard', 'tp'), may hold values from -0.1875 to 0.1875
- bias_qv: float32 [2, 1024], P(None, 'tp'), may hold values from -3 to 3
- w_out: bfloat16 [1024, 1024], P('tp', 'shard'), may hold values from -0.75 to 0.75
- bias_out: float32 [1024], replicated, may hold values from -3 to 3
- norm1_gain: float32 [1024], replicated, may hold values from 0.5 to 1.5
- norm1_shift: float32 [1024], replicated, may hold values from -3 to 3
- w_up: bfloat16 [1024, 4096], P('shard', 'tp'), may hold values from -0.1875 to 0.1875
- bias_up: float32 [4096], P('tp'), may hold values from -3 to 3
- w_down: bfloat16 [4096, 1024], P('tp', 'shard'), may hold values from -0.09375 to 0.09375
- bias_down: float32 [1024], replicated, may hold values from -3 to 3
- norm2_gain: float32 [1024], replicated, may hold values from 0.5 to 1.5
- norm2_shift: float32 [1024], replicated, may hold values from -3 to 3
Outputs:
- output: bfloat16 [4, 1024, 1024], P('shard', 'ctx')
- input_grad: bfloat16 [4, 1024, 1024], P('shard', 'ctx')
- w_qkv_grad: float32 [3, 1024, 1024], P(None, 'shard', 'tp')
- bias_qv_grad: float32 [2, 1024], P(None, 'tp')
- w_out_grad: float32 [1024, 1024], P('tp', 'shard')
- bias_out_grad: float32 [1024], replicated
- norm1_gain_grad: float32 [1024], replicated
- norm1_shift_grad: float32 [1024], replicated
- w_up_grad: float32 [1024, 4096], P('shard', 'tp')
- bias_up_grad: float32 [4096], P('tp')
- w_down_grad: float32 [4096, 1024], P('tp', 'shard')
- bias_down_grad: float32 [1024], replicated
- norm2_gain_grad: float32 [1024], replicated
- norm2_shift_grad: float32 [1024], replicated
The draws below stay inside these ranges and needn't reach their ends.
Inputs may be any that keep to these rules, and one draw needn't show every extreme that they name: `segment_ids`: within each sequence the ids never fall and start at 0; each document has at most 512 tokens, and some document has exactly that many.
All inputs are finite; a program needn't handle non-finite values.
Results may differ from the reference program's by a relative error of at most 0.022.
The reference program's roundings to bfloat16 on the way count: a program that leaves them out, or rounds other values in their place, can miss the bound.
Values may be sent and summed in bfloat16 or wider, within the bound.
A program may use at most 128 MiB of HBM per device.

```python
import math
import jax
import jax.numpy as jnp
import numpy as np
from jax import lax

D = 1024
FF = 4096
HEADS = 16
SEQ = 1024
HEAD_DIM = 64
NSEQ = 4


def draw_hidden_in(key, part):
    drawn = jax.random.truncated_normal(jax.random.fold_in(key, 1), -6.0, 6.0, (NSEQ, SEQ, D), jnp.float32)
    return drawn.astype(jnp.bfloat16)


def draw_w_qkv(key, part):
    drawn = jax.random.truncated_normal(jax.random.fold_in(key, 11), -6.0, 6.0, (3, D, D), jnp.float32) * D ** (-0.5)
    return drawn.astype(jnp.bfloat16)


def level_of(own_key, shape, shards, smallest, top_value):
    def one(axis_at, blocks):
        heights = jax.random.uniform(jax.random.fold_in(jax.random.fold_in(own_key, 6), axis_at), (blocks,), jnp.float32, smallest / len(shards), top_value / len(shards))
        return jnp.repeat(jnp.exp(heights), shape[axis_at] // blocks).reshape((-1,) + (1,) * (len(shape) - axis_at - 1))

    level = one(*shards[0])
    for cut in shards[1:]:
        level = level * one(*cut)
    return level


def length_profile(count, total, most, skew):
    portions = [(1 << 20) // math.isqrt(grade ** skew) + 1 for grade in range(2, count + 1)]
    spare, counts = total - most - (count - 1), [1] * (count - 1)
    while spare > 0:
        movable = [i for i in range(count - 1) if counts[i] < most]
        whole, left = sum([portions[i] for i in movable]), spare
        for i in movable:
            extra = min(most - counts[i], max(1, left * portions[i] // whole), spare)
            counts[i] = counts[i] + extra
            spare = spare - extra
    return np.array([most] + counts)


def ragged(key, count, total, bound, skew):
    if count == 2:
        one = jax.random.randint(key, (), max(1, total - bound), min(bound, total - 1) + 1)
        return jnp.stack([one, total - one])
    lengths = jnp.asarray(length_profile(count, total, bound, skew), jnp.int32)
    pairs = (count - 1) // 2
    donor, receiver = lengths[1:1 + 2 * pairs:2], lengths[2:2 + 2 * pairs:2]
    room = jnp.minimum(donor - 1, bound - receiver)
    moved = jax.random.randint(jax.random.fold_in(key, 1), (pairs,), 0, 1 << 20) % (room + 1)
    lengths = lengths.at[1:1 + 2 * pairs:2].set(donor - moved).at[2:2 + 2 * pairs:2].set(receiver + moved)
    return lengths[jax.random.permutation(jax.random.fold_in(key, 2), count)]


def bell_draw(rng, extent, width, reach, split=(), kind=jnp.bfloat16):
    factor_of = level_of(rng, extent, split, -0.22, 0.18) if split else 1.0
    array = jax.random.normal(rng, extent, jnp.float32) * width * factor_of
    return jnp.minimum(jnp.maximum(array, -reach), reach).astype(kind)


def setup_inputs(seed: int = 0) -> dict:
    key_list = jax.random.split(jax.random.key(seed), 16)
    return {
        "hidden_in": draw_hidden_in(jax.random.fold_in(key_list[15], 71), 0),
        "out_grad": bell_draw(key_list[1], (NSEQ, SEQ, D), 1.0, 6.0, ((0, 4), (1, 4))),
        "segment_ids": jax.vmap(lambda own: jnp.searchsorted(jnp.cumsum(ragged(own, 4, SEQ, SEQ // 2, 1)), jnp.arange(SEQ), side="right"))(jax.random.split(key_list[2], NSEQ)).reshape((NSEQ, SEQ)).astype(jnp.int32),
        "w_qkv": draw_w_qkv(jax.random.fold_in(key_list[15], 71), 0),
        "bias_qv": bell_draw(key_list[4], (2, D), 0.5, 3.0, ((1, 2),), jnp.float32),
        "w_out": bell_draw(key_list[5], (D, D), (D // 16) ** -0.5, 0.75, ((0, 2), (1, 4))),
        "bias_out": bell_draw(key_list[6], (D,), 0.5, 3.0, (), jnp.float32),
        "norm1_gain": jnp.clip(1.0 + 0.1 * jax.random.normal(key_list[7], (D,), jnp.float32), 0.5, 1.5),
        "norm1_shift": bell_draw(key_list[8], (D,), 0.5, 3.0, (), jnp.float32),
        "w_up": bell_draw(key_list[9], (D, FF), D ** -0.5, 0.1875, ((0, 4), (1, 2))),
        "bias_up": bell_draw(key_list[10], (FF,), 0.5, 3.0, ((0, 2),), jnp.float32),
        "w_down": bell_draw(key_list[11], (FF, D), FF ** -0.5, 0.09375, ((0, 2), (1, 4))),
        "bias_down": bell_draw(key_list[12], (D,), 0.5, 3.0, (), jnp.float32),
        "norm2_gain": jnp.clip(1.0 + 0.1 * jax.random.normal(key_list[13], (D,), jnp.float32), 0.5, 1.5),
        "norm2_shift": bell_draw(key_list[14], (D,), 0.5, 3.0, (), jnp.float32),
    }


EPSILON = 1e-05

def normalize(resid, gain, shift):
    average = lax.optimization_barrier(jnp.mean(resid, axis=-1, keepdims=True))
    centred = resid - average
    variance = lax.optimization_barrier(jnp.mean(centred * centred, axis=-1, keepdims=True))
    inv_std = lax.rsqrt(variance + EPSILON)
    normed = centred * inv_std
    return (normed * gain + shift, normed, inv_std)

def normalize_back(cotan, normed, inv_std, gain):
    scaled = cotan * gain
    return inv_std * (scaled - lax.optimization_barrier(jnp.mean(scaled, axis=-1, keepdims=True)) - normed * lax.optimization_barrier(jnp.mean(scaled * normed, axis=-1, keepdims=True)))

def gelu_value(pre_act):
    return 0.5 * pre_act * (1.0 + jax.scipy.special.erf(pre_act * 0.7071067811865476))

def gelu_slope(pre_act):
    return 0.5 * (1.0 + jax.scipy.special.erf(pre_act * 0.7071067811865476)) + pre_act * jnp.exp(-0.5 * pre_act * pre_act) * 0.3989422804014327

def reference(hidden_in, out_grad, segment_ids, w_qkv, bias_qv, w_out, bias_out, norm1_gain, norm1_shift, w_up, bias_up, w_down, bias_down, norm2_gain, norm2_shift):
    scale = 1.0 / math.sqrt(HEAD_DIM)
    qkv_float = w_qkv.astype(jnp.float32)
    bias_three = jnp.stack([bias_qv[0], jnp.zeros((D,), jnp.float32), bias_qv[1]]).astype(jnp.float32)

    def one_sequence(totals, inputs):
        tokens, cotangent, seq_ids = inputs
        tok_float = tokens.astype(jnp.float32)
        project = jnp.einsum('td,kde->kte', tok_float, qkv_float) + bias_three[:, None, :]
        project = lax.optimization_barrier(project.astype(jnp.bfloat16))
        heads = project.reshape(3, SEQ, HEADS, HEAD_DIM).astype(jnp.float32)
        query, keys, values = (heads[0], heads[1], heads[2])
        same_doc = seq_ids[:, None] == seq_ids[None, :]
        scores = jnp.einsum('qhe,khe->hqk', query, keys) * scale
        scores = jnp.where(same_doc[None], scores, -jnp.inf)
        log_total = jax.nn.logsumexp(scores, axis=-1)
        probs = jnp.exp(scores - log_total[..., None])
        probs_low = lax.optimization_barrier(probs.astype(jnp.bfloat16)).astype(jnp.float32)
        attended = jnp.einsum('hqk,khe->qhe', probs_low, values).astype(jnp.bfloat16)
        attended_flat = attended.reshape(SEQ, D)
        resid_one = jnp.dot(attended_flat, w_out, preferred_element_type=jnp.float32) + bias_out + tok_float
        first, normed_one, inv_one = normalize(resid_one, norm1_gain, norm1_shift)
        first_low = first.astype(jnp.bfloat16)
        pre_act = jnp.dot(first_low, w_up, preferred_element_type=jnp.float32) + bias_up
        activated = gelu_value(pre_act).astype(jnp.bfloat16)
        resid_two = jnp.dot(activated, w_down, preferred_element_type=jnp.float32) + bias_down + first
        result, normed_two, inv_two = normalize(resid_two, norm2_gain, norm2_shift)
        grad_float = cotangent.astype(jnp.float32)
        gain_two_grad = lax.optimization_barrier(jnp.sum(grad_float * normed_two, axis=0))
        shift_two_grad = lax.optimization_barrier(jnp.sum(grad_float, axis=0))
        resid_two_grad = normalize_back(grad_float, normed_two, inv_two, norm2_gain)
        resid_two_low = resid_two_grad.astype(jnp.bfloat16)
        down_grad = jnp.dot(activated.T, resid_two_low, preferred_element_type=jnp.float32)
        bias_down_grad = lax.optimization_barrier(jnp.sum(resid_two_grad, axis=0))
        act_grad = jnp.dot(resid_two_low, w_down.T, preferred_element_type=jnp.float32)
        pre_grad = act_grad * gelu_slope(pre_act)
        pre_low = pre_grad.astype(jnp.bfloat16)
        up_grad = jnp.dot(first_low.T, pre_low, preferred_element_type=jnp.float32)
        bias_up_grad = lax.optimization_barrier(jnp.sum(pre_grad, axis=0))
        first_grad = resid_two_grad + jnp.dot(pre_low, w_up.T, preferred_element_type=jnp.float32)
        gain_one_grad = lax.optimization_barrier(jnp.sum(first_grad * normed_one, axis=0))
        shift_one_grad = lax.optimization_barrier(jnp.sum(first_grad, axis=0))
        resid_one_grad = normalize_back(first_grad, normed_one, inv_one, norm1_gain)
        resid_one_low = resid_one_grad.astype(jnp.bfloat16)
        out_weight_grad = jnp.dot(attended_flat.T, resid_one_low, preferred_element_type=jnp.float32)
        bias_out_grad = lax.optimization_barrier(jnp.sum(resid_one_grad, axis=0))
        attended_grad = jnp.dot(resid_one_low, w_out.T, preferred_element_type=jnp.float32).astype(jnp.bfloat16)
        att_grad_float = attended_grad.reshape(SEQ, HEADS, HEAD_DIM).astype(jnp.float32)
        prob_grad = jnp.einsum('qhe,khe->hqk', att_grad_float, values)
        offset = lax.optimization_barrier(jnp.sum(att_grad_float * attended.astype(jnp.float32), axis=-1)).T
        score_grad = (probs * (prob_grad - offset[..., None]) * scale).astype(jnp.bfloat16)
        score_grad = lax.optimization_barrier(score_grad).astype(jnp.float32)
        query_grad = jnp.einsum('hqk,khe->qhe', score_grad, keys).astype(jnp.bfloat16)
        key_grad = jnp.einsum('hqk,qhe->khe', score_grad, query).astype(jnp.bfloat16)
        value_grad = jnp.einsum('hqk,qhe->khe', probs_low, att_grad_float).astype(jnp.bfloat16)
        proj_grad = jnp.stack([query_grad, key_grad, value_grad]).reshape(3, SEQ, D).astype(jnp.float32)
        qkv_grad = jnp.einsum('td,kte->kde', tok_float, proj_grad)
        bias_qv_grad = jnp.stack([lax.optimization_barrier(jnp.sum(proj_grad[0], axis=0)), lax.optimization_barrier(jnp.sum(proj_grad[2], axis=0))])
        input_grad = (resid_one_grad + jnp.einsum('kte,kde->td', proj_grad, qkv_float)).astype(jnp.bfloat16)
        terms = (qkv_grad, bias_qv_grad, out_weight_grad, bias_out_grad, gain_one_grad, shift_one_grad, up_grad, bias_up_grad, down_grad, bias_down_grad, gain_two_grad, shift_two_grad)
        totals = tuple((total + term for total, term in zip(totals, terms)))
        return (totals, (result.astype(jnp.bfloat16), input_grad))
    zeros_init = (jnp.zeros((3, D, D), jnp.float32), jnp.zeros((2, D), jnp.float32), jnp.zeros((D, D), jnp.float32), jnp.zeros((D,), jnp.float32), jnp.zeros((D,), jnp.float32), jnp.zeros((D,), jnp.float32), jnp.zeros((D, FF), jnp.float32), jnp.zeros((FF,), jnp.float32), jnp.zeros((FF, D), jnp.float32), jnp.zeros((D,), jnp.float32), jnp.zeros((D,), jnp.float32), jnp.zeros((D,), jnp.float32))
    totals, (output, input_grad) = lax.scan(one_sequence, zeros_init, (hidden_in, out_grad, segment_ids))
    return (output, input_grad, totals[0], totals[1], totals[2], totals[3], totals[4], totals[5], totals[6], totals[7], totals[8], totals[9], totals[10], totals[11])
```

```python
import math

import jax
import jax.numpy as jnp
from jax import lax
from jax.sharding import PartitionSpec as P

HEADS = 16


EPSILON = 1e-05


def normalize(resid, gain, shift):
    average = jnp.mean(resid, axis=-1, keepdims=True)
    centred = resid - average
    variance = jnp.mean(centred * centred, axis=-1, keepdims=True)
    inv_std = lax.rsqrt(variance + EPSILON)
    normed = centred * inv_std
    return (normed * gain + shift, normed, inv_std)


def normalize_back(cotan, normed, inv_std, gain):
    scaled = cotan * gain
    return inv_std * (
        scaled
        - jnp.mean(scaled, axis=-1, keepdims=True)
        - normed * jnp.mean(scaled * normed, axis=-1, keepdims=True)
    )


def gelu_value(pre_act):
    return 0.5 * pre_act * (1.0 + jax.scipy.special.erf(pre_act * 0.7071067811865476))


def gelu_slope(pre_act):
    return (
        0.5 * (1.0 + jax.scipy.special.erf(pre_act * 0.7071067811865476))
        + pre_act * jnp.exp(-0.5 * pre_act * pre_act) * 0.3989422804014327
    )


def block_scores(query_block, keys, ids_block, ids_whole, scale):
    scores = (
        jnp.einsum("qhe,khe->hqk", query_block, keys, preferred_element_type=jnp.float32) * scale
    )
    return jnp.where((ids_block[:, None] == ids_whole[None, :])[None], scores, -jnp.inf)


GROUP = ("ctx", "tp")


def dot_t(left, right):
    return lax.dot_general(
        left, right, (((1,), (1,)), ((), ())), preferred_element_type=jnp.float32
    )


def dot_rows(left, right):
    return lax.dot_general(
        left, right, (((0,), (0,)), ((), ())), preferred_element_type=jnp.float32
    )


def dot(left, right):
    return jnp.dot(left, right, preferred_element_type=jnp.float32)


def spread(part):
    return lax.all_gather(part, GROUP, axis=1, tiled=True)


def collect(whole):
    return lax.psum_scatter(whole, GROUP, scatter_dimension=1, tiled=True).astype(jnp.float32)


def shards(
    hidden_in,
    out_grad,
    segment_ids,
    w_qkv,
    bias_qv,
    w_out,
    bias_out,
    norm1_gain,
    norm1_shift,
    w_up,
    bias_up,
    w_down,
    bias_down,
    norm2_gain,
    norm2_shift,
):
    seq_count, local_len, width = hidden_in.shape
    ctx_count = lax.axis_size("ctx")
    tp_count = lax.axis_size("tp")
    ctx_at = lax.axis_index("ctx")
    tp_at = lax.axis_index("tp")
    full_len = local_len * ctx_count
    part_len = local_len // tp_count
    row_count = seq_count * full_len
    head_dim = width // HEADS
    scale = 1.0 / math.sqrt(head_dim)
    owned_rows = w_up.shape[0]
    cols = w_qkv.shape[2] // ctx_count
    units = w_up.shape[1] // ctx_count
    local_heads = cols // head_dim
    block_rows = min(512, full_len)
    block_count = full_len // block_rows

    def mine(array, size, axis):
        return lax.dynamic_slice_in_dim(array, ctx_at * size, size, axis)

    qkv_own = mine(w_qkv, cols, 2).transpose(1, 0, 2).reshape(owned_rows, 3 * cols)
    qkv_full = lax.all_gather(qkv_own, "shard", axis=0, tiled=True)
    tokens_all = lax.all_gather(hidden_in, "ctx", axis=1, tiled=True).reshape(row_count, width)
    rest_own = jnp.concatenate(
        [mine(w_out, cols, 0).T, mine(w_up, units, 1), mine(w_down, units, 0).T], axis=1
    )
    rest_full = lax.all_gather(rest_own, "shard", axis=0, tiled=True)
    out_full = rest_full[:, :cols]
    up_full = rest_full[:, cols : cols + units]
    down_full = rest_full[:, cols + units :]

    bias_own = mine(bias_qv, cols, 1)
    bias_three = jnp.concatenate([bias_own[0], jnp.zeros_like(bias_own[0]), bias_own[1]])
    project = (dot(tokens_all, qkv_full) + bias_three).astype(jnp.bfloat16)
    heads = project.reshape(seq_count, full_len, 3, local_heads, head_dim)

    def attend_sequence(packed):
        seq_heads, seq_ids = packed
        keys = seq_heads[:, 1]
        values = seq_heads[:, 2]
        queries = seq_heads[:, 0].reshape(block_count, block_rows, local_heads, head_dim)
        id_blocks = seq_ids.reshape(block_count, block_rows)

        def attend_block(piece):
            query_block, ids_block = piece
            scores = block_scores(query_block, keys, ids_block, seq_ids, scale)
            log_total = jax.nn.logsumexp(scores, axis=-1)
            probs_low = jnp.exp(scores - log_total[..., None]).astype(jnp.bfloat16)
            attended = jnp.einsum(
                "hqk,khe->qhe", probs_low, values, preferred_element_type=jnp.float32
            ).astype(jnp.bfloat16)
            return (attended, log_total)

        attended, log_total = lax.map(attend_block, (queries, id_blocks))
        return (attended.reshape(full_len, local_heads, head_dim), log_total)

    attended_heads, log_totals = lax.map(attend_sequence, (heads, segment_ids))
    attended = attended_heads.reshape(row_count, cols)

    def whole(part):
        return part.astype(jnp.bfloat16).reshape(seq_count, full_len, width)

    def part_of(array):
        return lax.dynamic_slice_in_dim(array, tp_at * part_len, part_len, 1)

    resid_one = (
        collect(whole(dot_t(attended, out_full)))
        + bias_out
        + part_of(hidden_in).astype(jnp.float32)
    )
    first, normed_one, inv_one = normalize(resid_one, norm1_gain, norm1_shift)
    first_all = spread(first.astype(jnp.bfloat16)).reshape(row_count, width)
    pre_act = dot(first_all, up_full) + mine(bias_up, units, 0)
    activated = gelu_value(pre_act).astype(jnp.bfloat16)
    resid_two = collect(whole(dot_t(activated, down_full))) + bias_down + first
    result, normed_two, inv_two = normalize(resid_two, norm2_gain, norm2_shift)
    grad_float = part_of(out_grad).astype(jnp.float32)

    def total(array):
        return jnp.sum(array, axis=(0, 1))

    gain_two_grad = total(grad_float * normed_two)
    shift_two_grad = total(grad_float)
    resid_two_grad = normalize_back(grad_float, normed_two, inv_two, norm2_gain)
    two_all = spread(resid_two_grad.astype(jnp.bfloat16)).reshape(row_count, width)
    output = lax.all_gather(result.astype(jnp.bfloat16), "tp", axis=1, tiled=True)
    bias_down_grad = total(resid_two_grad)
    pre_grad = dot(two_all, down_full) * gelu_slope(pre_act)
    pre_low = pre_grad.astype(jnp.bfloat16)
    bias_up_grad = jnp.sum(pre_grad, axis=0)
    first_grad = resid_two_grad + collect(whole(dot_t(pre_low, up_full)))
    part_ffn = jnp.concatenate(
        [dot_rows(first_all, pre_low), dot_rows(two_all, activated)], axis=1
    ).astype(jnp.bfloat16)
    gain_one_grad = total(first_grad * normed_one)
    shift_one_grad = total(first_grad)
    resid_one_grad = normalize_back(first_grad, normed_one, inv_one, norm1_gain)
    bias_out_grad = total(resid_one_grad)
    one_all = spread(resid_one_grad.astype(jnp.bfloat16)).reshape(row_count, width)
    attended_grad = dot(one_all, out_full).astype(jnp.bfloat16)
    grad_heads = attended_grad.reshape(seq_count, full_len, local_heads, head_dim)

    def back_sequence(packed):
        seq_heads, seq_ids, seq_attended, seq_grad, seq_log = packed
        keys = seq_heads[:, 1]
        values = seq_heads[:, 2]
        queries = seq_heads[:, 0].reshape(block_count, block_rows, local_heads, head_dim)
        id_blocks = seq_ids.reshape(block_count, block_rows)
        att_blocks = seq_attended.reshape(block_count, block_rows, local_heads, head_dim)
        grad_blocks = seq_grad.reshape(block_count, block_rows, local_heads, head_dim)

        def back_block(carry, piece):
            key_total, value_total = carry
            query_block, ids_block, att_block, grad_block, log_block = piece
            scores = block_scores(query_block, keys, ids_block, seq_ids, scale)
            probs = jnp.exp(scores - log_block[..., None])
            probs_low = probs.astype(jnp.bfloat16)
            prob_grad = jnp.einsum(
                "qhe,khe->hqk", grad_block, values, preferred_element_type=jnp.float32
            )
            offset = jnp.sum(
                grad_block.astype(jnp.float32) * att_block.astype(jnp.float32), axis=-1
            ).T
            score_grad = (probs * (prob_grad - offset[..., None]) * scale).astype(jnp.bfloat16)
            query_grad = jnp.einsum(
                "hqk,khe->qhe", score_grad, keys, preferred_element_type=jnp.float32
            ).astype(jnp.bfloat16)
            key_total = key_total + jnp.einsum(
                "hqk,qhe->khe", score_grad, query_block, preferred_element_type=jnp.float32
            )
            value_total = value_total + jnp.einsum(
                "hqk,qhe->khe", probs_low, grad_block, preferred_element_type=jnp.float32
            )
            return ((key_total, value_total), query_grad)

        empty = jnp.zeros((full_len, local_heads, head_dim), jnp.float32)
        (key_total, value_total), query_grads = lax.scan(
            back_block, (empty, empty), (queries, id_blocks, att_blocks, grad_blocks, seq_log)
        )
        return jnp.stack(
            [
                query_grads.reshape(full_len, local_heads, head_dim),
                key_total.astype(jnp.bfloat16),
                value_total.astype(jnp.bfloat16),
            ],
            axis=1,
        )

    head_grads = lax.map(
        back_sequence, (heads, segment_ids, attended_heads, grad_heads, log_totals)
    )
    proj_grad = head_grads.reshape(row_count, 3 * cols)
    proj_sum = jnp.sum(proj_grad.astype(jnp.float32), axis=0)
    bias_qv_grad = jnp.concatenate([proj_sum[:cols], proj_sum[2 * cols :]])
    input_part = resid_one_grad + collect(whole(dot_t(proj_grad, qkv_full)))
    input_grad = lax.all_gather(input_part.astype(jnp.bfloat16), "tp", axis=1, tiled=True)
    part_attn = jnp.concatenate(
        [dot_rows(tokens_all, proj_grad), dot_rows(one_all, attended)], axis=1
    ).astype(jnp.bfloat16)

    def owned(part):
        mean = lax.psum_scatter(part, "shard", scatter_dimension=0, tiled=True)
        return lax.all_gather(mean, "ctx", axis=0).astype(jnp.float32)

    own_ffn = owned(part_ffn)
    own_attn = owned(part_attn)
    up_grad = own_ffn[:, :, :units].transpose(1, 0, 2).reshape(w_up.shape)
    down_grad = own_ffn[:, :, units:].transpose(0, 2, 1).reshape(w_down.shape)
    qkv_grad = (
        own_attn[:, :, : 3 * cols]
        .reshape(ctx_count, owned_rows, 3, cols)
        .transpose(2, 1, 0, 3)
        .reshape(w_qkv.shape)
    )
    out_weight_grad = own_attn[:, :, 3 * cols :].transpose(0, 2, 1).reshape(w_out.shape)
    sliced = jnp.concatenate([bias_qv_grad, bias_up_grad])
    slots = jnp.zeros((tp_count, ctx_count, sliced.shape[0]), jnp.float32)
    slots = lax.dynamic_update_slice(slots, sliced[None, None], (tp_at, ctx_at, 0))
    small = lax.psum(
        jnp.concatenate(
            [
                bias_out_grad,
                gain_one_grad,
                shift_one_grad,
                bias_down_grad,
                gain_two_grad,
                shift_two_grad,
                slots.reshape(-1),
            ]
        ),
        ("shard", "ctx", "tp"),
    )
    sums = small[: 6 * width].reshape(6, width)
    slots = small[6 * width :].reshape(tp_count, ctx_count, -1)
    slots = lax.dynamic_index_in_dim(slots, tp_at, 0, keepdims=False)
    bias_qv_total = (
        slots[:, : 2 * cols].reshape(ctx_count, 2, cols).transpose(1, 0, 2).reshape(bias_qv.shape)
    )
    return (
        output,
        input_grad,
        qkv_grad,
        bias_qv_total,
        out_weight_grad,
        sums[0],
        sums[1],
        sums[2],
        up_grad,
        slots[:, 2 * cols :].reshape(bias_up.shape),
        down_grad,
        sums[3],
        sums[4],
        sums[5],
    )


def solution(mesh):
    return jax.shard_map(
        shards,
        mesh=mesh,
        in_specs=(
            P("shard", "ctx", None),
            P("shard", "ctx", None),
            P("shard", None),
            P(None, "shard", "tp"),
            P(None, "tp"),
            P("tp", "shard"),
            P(),
            P(),
            P(),
            P("shard", "tp"),
            P("tp"),
            P("tp", "shard"),
            P(),
            P(),
            P(),
        ),
        out_specs=(
            P("shard", "ctx", None),
            P("shard", "ctx", None),
            P(None, "shard", "tp"),
            P(None, "tp"),
            P("tp", "shard"),
            P(),
            P(),
            P(),
            P("shard", "tp"),
            P("tp"),
            P("tp", "shard"),
            P(),
            P(),
            P(),
        ),
        check_vma=False,
    )
```

```python
import functools
import math

import jax
import jax.numpy as jnp
from jax import lax
from jax.experimental import pallas as pl
from jax.experimental.pallas import tpu as pltpu
from jax.sharding import PartitionSpec as P

HEADS = 16


EPSILON = 1e-05


def normalize(resid, gain, shift):
    average = jnp.mean(resid, axis=-1, keepdims=True)
    centred = resid - average
    variance = jnp.mean(centred * centred, axis=-1, keepdims=True)
    inv_std = lax.rsqrt(variance + EPSILON)
    normed = centred * inv_std
    return (normed * gain + shift, normed, inv_std)


def normalize_back(cotan, normed, inv_std, gain):
    scaled = cotan * gain
    return inv_std * (
        scaled
        - jnp.mean(scaled, axis=-1, keepdims=True)
        - normed * jnp.mean(scaled * normed, axis=-1, keepdims=True)
    )


def gelu_value(pre_act):
    return 0.5 * pre_act * (1.0 + jax.scipy.special.erf(pre_act * 0.7071067811865476))


def gelu_slope(pre_act):
    return (
        0.5 * (1.0 + jax.scipy.special.erf(pre_act * 0.7071067811865476))
        + pre_act * jnp.exp(-0.5 * pre_act * pre_act) * 0.3989422804014327
    )


def block_scores(query_block, keys, ids_block, ids_whole, scale):
    scores = (
        jnp.einsum("qhe,khe->hqk", query_block, keys, preferred_element_type=jnp.float32) * scale
    )
    return jnp.where((ids_block[:, None] == ids_whole[None, :])[None], scores, -jnp.inf)


def dot_t(left, right):
    return lax.dot_general(
        left, right, (((1,), (1,)), ((), ())), preferred_element_type=jnp.float32
    )


def dot_rows(left, right):
    return lax.dot_general(
        left, right, (((0,), (0,)), ((), ())), preferred_element_type=jnp.float32
    )


def dot(left, right):
    return jnp.dot(left, right, preferred_element_type=jnp.float32)


MESH = pl.DeviceIdType.MESH


def places(tp_count, chip_count):
    ctx_at = lax.axis_index("ctx")
    tp_at = lax.axis_index("tp")
    core = ctx_at % 2
    chip = (ctx_at // 2) * tp_count + tp_at

    def slot(at, own):
        return ((at // tp_count) * 2 + own) * tp_count + at % tp_count

    def device(at, own):
        return {"ctx": (at // tp_count) * 2 + own, "tp": at % tp_count}

    others = [(chip + step) % chip_count for step in range(chip_count)]
    return chip, core, slot, device, others


def greet(core, device, others):
    barrier = pltpu.get_barrier_semaphore()
    for step, other in enumerate(others):
        target = device(other, core) if step else device(other, 1 - core)
        pl.semaphore_signal(barrier, inc=1, device_id=target, device_id_type=MESH)
    pl.semaphore_wait(barrier, len(others))


def remote(src, dst, sems, step, target):
    return pltpu.make_async_remote_copy(
        src_ref=src,
        dst_ref=dst,
        send_sem=sems[0].at[step],
        recv_sem=sems[1].at[step],
        device_id=target,
        device_id_type=MESH,
    )


def spread_kernel(
    tp_count, chip_count, own_ref, all_ref, far_send, far_recv, near_send, near_recv, keep_sem
):
    chip, core, slot, device, others = places(tp_count, chip_count)
    far, near = (far_send, far_recv), (near_send, near_recv)
    greet(core, device, others)
    mine = all_ref.at[slot(chip, core)]
    far_copies = [
        remote(own_ref, mine, far, step, device(others[step], core))
        for step in range(1, chip_count)
    ]
    for copy in far_copies:
        copy.start()
    partner = device(chip, 1 - core)
    near_copies = [remote(own_ref, mine, near, 0, partner)]
    near_copies[0].start()
    keep = pltpu.make_async_copy(own_ref, mine, keep_sem)
    keep.start()
    for step in range(1, chip_count):
        far_copies[step - 1].wait_recv()
        source = (chip + chip_count - step) % chip_count
        block = all_ref.at[slot(source, core)]
        copy = remote(block, block, near, step, partner)
        copy.start()
        near_copies.append(copy)
    keep.wait()
    for copy in far_copies:
        copy.wait_send()
    for copy in near_copies:
        copy.wait()


def collect_kernel(
    tp_count,
    chip_count,
    part_ref,
    sum_ref,
    near_buf,
    stage,
    far_buf,
    far_send,
    far_recv,
    near_send,
    near_recv,
):
    chip, core, slot, device, others = places(tp_count, chip_count)
    far, near = (far_send, far_recv), (near_send, near_recv)
    greet(core, device, others)
    partner = device(chip, 1 - core)
    order = list(range(1, chip_count)) + [0]
    near_copies = {}
    for step in order:
        block = part_ref.at[slot(others[step], 1 - core)]
        near_copies[step] = remote(block, near_buf.at[step], near, step, partner)
        near_copies[step].start()
    far_copies = {}
    for step in order:
        near_copies[step].wait_recv()
        both = part_ref[slot(others[step], core)].astype(jnp.float32) + near_buf[step].astype(
            jnp.float32
        )
        if step:
            stage[step] = both.astype(stage.dtype)
            far_copies[step] = remote(
                stage.at[step], far_buf.at[step], far, step, device(others[step], core)
            )
            far_copies[step].start()
        else:
            sum_ref[...] = both
    for step in range(1, chip_count):
        far_copies[step].wait_recv()
        sum_ref[...] += far_buf[step].astype(jnp.float32)
    for step in range(1, chip_count):
        far_copies[step].wait_send()
    for step in order:
        near_copies[step].wait_send()


def group_sizes():
    tp_count = lax.axis_size("tp")
    slots = lax.axis_size("ctx") * tp_count
    return tp_count, slots, slots // 2


def spread(part):
    seq_count, part_len, width = part.shape
    tp_count, slots, chips = group_sizes()
    rows = seq_count * part_len
    gathered = pl.pallas_call(
        functools.partial(spread_kernel, tp_count, chips),
        out_shape=jax.ShapeDtypeStruct((slots, rows, width), part.dtype),
        in_specs=[pl.BlockSpec(memory_space=pltpu.VMEM)],
        out_specs=pl.BlockSpec(memory_space=pltpu.VMEM),
        scratch_shapes=[pltpu.SemaphoreType.DMA((chips,))] * 4 + [pltpu.SemaphoreType.DMA],
        compiler_params=pltpu.CompilerParams(collective_id=0, has_side_effects=True),
        name="spread",
    )(part.reshape(rows, width))
    return gathered.reshape(slots, seq_count, part_len, width).transpose(1, 0, 2, 3)


def collect(whole):
    seq_count, full_len, width = whole.shape
    tp_count, slots, chips = group_sizes()
    part_len = full_len // slots
    rows = seq_count * part_len
    blocks = whole.reshape(seq_count, slots, part_len, width).transpose(1, 0, 2, 3)
    buffer = pltpu.VMEM((chips, rows, width), whole.dtype)
    return pl.pallas_call(
        functools.partial(collect_kernel, tp_count, chips),
        out_shape=jax.ShapeDtypeStruct((rows, width), jnp.float32),
        in_specs=[pl.BlockSpec(memory_space=pltpu.VMEM)],
        out_specs=pl.BlockSpec(memory_space=pltpu.VMEM),
        scratch_shapes=[buffer] * 3 + [pltpu.SemaphoreType.DMA((chips,))] * 4,
        compiler_params=pltpu.CompilerParams(collective_id=1, has_side_effects=True),
        name="collect",
    )(blocks.reshape(slots, rows, width)).reshape(seq_count, part_len, width)


def shards(
    hidden_in,
    out_grad,
    segment_ids,
    w_qkv,
    bias_qv,
    w_out,
    bias_out,
    norm1_gain,
    norm1_shift,
    w_up,
    bias_up,
    w_down,
    bias_down,
    norm2_gain,
    norm2_shift,
):
    seq_count, local_len, width = hidden_in.shape
    ctx_count = lax.axis_size("ctx")
    tp_count = lax.axis_size("tp")
    ctx_at = lax.axis_index("ctx")
    tp_at = lax.axis_index("tp")
    full_len = local_len * ctx_count
    part_len = local_len // tp_count
    row_count = seq_count * full_len
    head_dim = width // HEADS
    scale = 1.0 / math.sqrt(head_dim)
    owned_rows = w_up.shape[0]
    cols = w_qkv.shape[2] // ctx_count
    units = w_up.shape[1] // ctx_count
    local_heads = cols // head_dim
    block_rows = min(512, full_len)
    block_count = full_len // block_rows

    def mine(array, size, axis):
        return lax.dynamic_slice_in_dim(array, ctx_at * size, size, axis)

    qkv_own = mine(w_qkv, cols, 2).transpose(1, 0, 2).reshape(owned_rows, 3 * cols)
    qkv_full = lax.all_gather(qkv_own, "shard", axis=0, tiled=True)
    tokens_all = lax.all_gather(hidden_in, "ctx", axis=1, tiled=True).reshape(row_count, width)
    rest_own = jnp.concatenate(
        [mine(w_out, cols, 0).T, mine(w_up, units, 1), mine(w_down, units, 0).T], axis=1
    )
    rest_full = lax.all_gather(rest_own, "shard", axis=0, tiled=True)
    out_full = rest_full[:, :cols]
    up_full = rest_full[:, cols : cols + units]
    down_full = rest_full[:, cols + units :]

    bias_own = mine(bias_qv, cols, 1)
    bias_three = jnp.concatenate([bias_own[0], jnp.zeros_like(bias_own[0]), bias_own[1]])
    project = (dot(tokens_all, qkv_full) + bias_three).astype(jnp.bfloat16)
    heads = project.reshape(seq_count, full_len, 3, local_heads, head_dim)

    def attend_sequence(packed):
        seq_heads, seq_ids = packed
        keys = seq_heads[:, 1]
        values = seq_heads[:, 2]
        queries = seq_heads[:, 0].reshape(block_count, block_rows, local_heads, head_dim)
        id_blocks = seq_ids.reshape(block_count, block_rows)

        def attend_block(piece):
            query_block, ids_block = piece
            scores = block_scores(query_block, keys, ids_block, seq_ids, scale)
            log_total = jax.nn.logsumexp(scores, axis=-1)
            probs_low = jnp.exp(scores - log_total[..., None]).astype(jnp.bfloat16)
            attended = jnp.einsum(
                "hqk,khe->qhe", probs_low, values, preferred_element_type=jnp.float32
            ).astype(jnp.bfloat16)
            return (attended, log_total)

        attended, log_total = lax.map(attend_block, (queries, id_blocks))
        return (attended.reshape(full_len, local_heads, head_dim), log_total)

    attended_heads, log_totals = lax.map(attend_sequence, (heads, segment_ids))
    attended = attended_heads.reshape(row_count, cols)

    def whole(part):
        return part.astype(jnp.bfloat16).reshape(seq_count, full_len, width)

    def part_of(array):
        return lax.dynamic_slice_in_dim(array, tp_at * part_len, part_len, 1)

    resid_one = (
        collect(whole(dot_t(attended, out_full)))
        + bias_out
        + part_of(hidden_in).astype(jnp.float32)
    )
    first, normed_one, inv_one = normalize(resid_one, norm1_gain, norm1_shift)
    first_all = spread(first.astype(jnp.bfloat16)).reshape(row_count, width)
    pre_act = dot(first_all, up_full) + mine(bias_up, units, 0)
    activated = gelu_value(pre_act).astype(jnp.bfloat16)
    resid_two = collect(whole(dot_t(activated, down_full))) + bias_down + first
    result, normed_two, inv_two = normalize(resid_two, norm2_gain, norm2_shift)
    grad_float = part_of(out_grad).astype(jnp.float32)

    def total(array):
        return jnp.sum(array, axis=(0, 1))

    gain_two_grad = total(grad_float * normed_two)
    shift_two_grad = total(grad_float)
    resid_two_grad = normalize_back(grad_float, normed_two, inv_two, norm2_gain)
    two_all = spread(resid_two_grad.astype(jnp.bfloat16)).reshape(row_count, width)
    output = lax.all_gather(result.astype(jnp.bfloat16), "tp", axis=1, tiled=True)
    bias_down_grad = total(resid_two_grad)
    pre_grad = dot(two_all, down_full) * gelu_slope(pre_act)
    pre_low = pre_grad.astype(jnp.bfloat16)
    bias_up_grad = jnp.sum(pre_grad, axis=0)
    first_grad = resid_two_grad + collect(whole(dot_t(pre_low, up_full)))
    part_ffn = jnp.concatenate(
        [dot_rows(first_all, pre_low), dot_rows(two_all, activated)], axis=1
    ).astype(jnp.bfloat16)
    gain_one_grad = total(first_grad * normed_one)
    shift_one_grad = total(first_grad)
    resid_one_grad = normalize_back(first_grad, normed_one, inv_one, norm1_gain)
    bias_out_grad = total(resid_one_grad)
    one_all = spread(resid_one_grad.astype(jnp.bfloat16)).reshape(row_count, width)
    attended_grad = dot(one_all, out_full).astype(jnp.bfloat16)
    grad_heads = attended_grad.reshape(seq_count, full_len, local_heads, head_dim)

    def back_sequence(packed):
        seq_heads, seq_ids, seq_attended, seq_grad, seq_log = packed
        keys = seq_heads[:, 1]
        values = seq_heads[:, 2]
        queries = seq_heads[:, 0].reshape(block_count, block_rows, local_heads, head_dim)
        id_blocks = seq_ids.reshape(block_count, block_rows)
        att_blocks = seq_attended.reshape(block_count, block_rows, local_heads, head_dim)
        grad_blocks = seq_grad.reshape(block_count, block_rows, local_heads, head_dim)

        def back_block(carry, piece):
            key_total, value_total = carry
            query_block, ids_block, att_block, grad_block, log_block = piece
            scores = block_scores(query_block, keys, ids_block, seq_ids, scale)
            probs = jnp.exp(scores - log_block[..., None])
            probs_low = probs.astype(jnp.bfloat16)
            prob_grad = jnp.einsum(
                "qhe,khe->hqk", grad_block, values, preferred_element_type=jnp.float32
            )
            offset = jnp.sum(
                grad_block.astype(jnp.float32) * att_block.astype(jnp.float32), axis=-1
            ).T
            score_grad = (probs * (prob_grad - offset[..., None]) * scale).astype(jnp.bfloat16)
            query_grad = jnp.einsum(
                "hqk,khe->qhe", score_grad, keys, preferred_element_type=jnp.float32
            ).astype(jnp.bfloat16)
            key_total = key_total + jnp.einsum(
                "hqk,qhe->khe", score_grad, query_block, preferred_element_type=jnp.float32
            )
            value_total = value_total + jnp.einsum(
                "hqk,qhe->khe", probs_low, grad_block, preferred_element_type=jnp.float32
            )
            return ((key_total, value_total), query_grad)

        empty = jnp.zeros((full_len, local_heads, head_dim), jnp.float32)
        (key_total, value_total), query_grads = lax.scan(
            back_block, (empty, empty), (queries, id_blocks, att_blocks, grad_blocks, seq_log)
        )
        return jnp.stack(
            [
                query_grads.reshape(full_len, local_heads, head_dim),
                key_total.astype(jnp.bfloat16),
                value_total.astype(jnp.bfloat16),
            ],
            axis=1,
        )

    head_grads = lax.map(
        back_sequence, (heads, segment_ids, attended_heads, grad_heads, log_totals)
    )
    proj_grad = head_grads.reshape(row_count, 3 * cols)
    proj_sum = jnp.sum(proj_grad.astype(jnp.float32), axis=0)
    bias_qv_grad = jnp.concatenate([proj_sum[:cols], proj_sum[2 * cols :]])
    input_part = resid_one_grad + collect(whole(dot_t(proj_grad, qkv_full)))
    input_grad = lax.all_gather(input_part.astype(jnp.bfloat16), "tp", axis=1, tiled=True)
    part_attn = jnp.concatenate(
        [dot_rows(tokens_all, proj_grad), dot_rows(one_all, attended)], axis=1
    ).astype(jnp.bfloat16)

    def owned(part):
        mean = lax.psum_scatter(part, "shard", scatter_dimension=0, tiled=True)
        return lax.all_gather(mean, "ctx", axis=0).astype(jnp.float32)

    own_ffn = owned(part_ffn)
    own_attn = owned(part_attn)
    up_grad = own_ffn[:, :, :units].transpose(1, 0, 2).reshape(w_up.shape)
    down_grad = own_ffn[:, :, units:].transpose(0, 2, 1).reshape(w_down.shape)
    qkv_grad = (
        own_attn[:, :, : 3 * cols]
        .reshape(ctx_count, owned_rows, 3, cols)
        .transpose(2, 1, 0, 3)
        .reshape(w_qkv.shape)
    )
    out_weight_grad = own_attn[:, :, 3 * cols :].transpose(0, 2, 1).reshape(w_out.shape)
    sliced = jnp.concatenate([bias_qv_grad, bias_up_grad])
    slots = jnp.zeros((tp_count, ctx_count, sliced.shape[0]), jnp.float32)
    slots = lax.dynamic_update_slice(slots, sliced[None, None], (tp_at, ctx_at, 0))
    small = lax.psum(
        jnp.concatenate(
            [
                bias_out_grad,
                gain_one_grad,
                shift_one_grad,
                bias_down_grad,
                gain_two_grad,
                shift_two_grad,
                slots.reshape(-1),
            ]
        ),
        ("shard", "ctx", "tp"),
    )
    sums = small[: 6 * width].reshape(6, width)
    slots = small[6 * width :].reshape(tp_count, ctx_count, -1)
    slots = lax.dynamic_index_in_dim(slots, tp_at, 0, keepdims=False)
    bias_qv_total = (
        slots[:, : 2 * cols].reshape(ctx_count, 2, cols).transpose(1, 0, 2).reshape(bias_qv.shape)
    )
    return (
        output,
        input_grad,
        qkv_grad,
        bias_qv_total,
        out_weight_grad,
        sums[0],
        sums[1],
        sums[2],
        up_grad,
        slots[:, 2 * cols :].reshape(bias_up.shape),
        down_grad,
        sums[3],
        sums[4],
        sums[5],
    )


def solution(mesh):
    return jax.shard_map(
        shards,
        mesh=mesh,
        in_specs=(
            P("shard", "ctx", None),
            P("shard", "ctx", None),
            P("shard", None),
            P(None, "shard", "tp"),
            P(None, "tp"),
            P("tp", "shard"),
            P(),
            P(),
            P(),
            P("shard", "tp"),
            P("tp"),
            P("tp", "shard"),
            P(),
            P(),
            P(),
        ),
        out_specs=(
            P("shard", "ctx", None),
            P("shard", "ctx", None),
            P(None, "shard", "tp"),
            P(None, "tp"),
            P("tp", "shard"),
            P(),
            P(),
            P(),
            P("shard", "tp"),
            P("tp"),
            P("tp", "shard"),
            P(),
            P(),
            P(),
        ),
        check_vma=False,
    )
```
